768 devices in a mesh: dp: 192 (over x, y, z_lo, core), seq: 4 (over z_hi).
Axes of the slice: x: 4, y: 8, z: 12 (z_hi: 4, z_lo: 3; z = z_hi * 3 + z_lo), core: 2. Of those that a mesh axis runs over, the one named last changes fastest.
Arguments:
- image_query: bfloat16 [192, 256, 1536], P('dp', 'seq'), may hold values from -300 to 300
- image_key: bfloat16 [192, 256, 1536], P('dp', 'seq'), may hold values from -300 to 300
- image_value: bfloat16 [192, 256, 1536], P('dp', 'seq'), may hold values from -6 to 6
- text_key: bfloat16 [192, 512, 1536], P('dp', 'seq'), may hold values from -300 to 300
- text_value: bfloat16 [192, 512, 1536], P('dp', 'seq'), may hold values from -6 to 6
- query_gain: float32 [128], replicated, may hold values from 0.6 to 1.8
- key_gain: float32 [128], replicated, may hold values from 0.6 to 1.8
- embed_weight: bfloat16 [1536, 1408], replicated, may hold values from -0.15625 to 0.15625
- position_embed: float32 [64, 1408], replicated, may hold values from -2.7 to 2.7
- norm_gain: float32 [1408], replicated, may hold values from 0.25 to 1.75
- final_gain: float32 [1408], replicated, may hold values from 0.25 to 1.75
- up_weight: bfloat16 [3072, 1408], P(('dp', 'seq')), may hold values from -0.15625 to 0.15625
- down_weight: bfloat16 [3072, 1408], P(('dp', 'seq')), may hold values from -0.109375 to 0.109375
- reward_direction: float32 [1408], replicated, may hold values from -1.5 to 1.5
Outputs:
- attended: bfloat16 [192, 256, 1536], P('dp', None, 'seq')
- attended_gradient: bfloat16 [192, 256, 1536], P('dp', None, 'seq')
- reward: float32 [192], P('dp')
The draws below stay inside these ranges and needn't reach their ends.
All inputs are finite; a program needn't handle non-finite values.
Results may differ from the reference program's by a relative error of at most 0.02.
Values may be sent and summed in bfloat16 or wider, within the bound.
No kernel may reach another device: no remote copies, remote signals or barrier semaphores. Data moves between devices by JAX's collectives and lax.ppermute only.
A program may use at most 64 MiB of HBM per device.

```python
import math
import jax
import jax.numpy as jnp
from jax import lax

HEAD = 128
HEADS = 12
HD = 1536
EMB = 1408
HID = 3072
PATCH_W = 32
BATCH = 192
IMG_TOK = 256
TXT_TOK = 512
REW_TOK = 64
N_DP = 192
N_SEQ = 4


def scaled_block(key, array_shape, base_entries, row_range, column_range):
    row_key, column_key = jax.random.split(key)
    row_shape = array_shape[:-1] + (1,)
    row_scale = jnp.exp(jax.random.uniform(row_key, row_shape, jnp.float32, math.log(row_range[0]), math.log(row_range[1])))
    column_scale = jnp.exp(jax.random.uniform(column_key, (array_shape[-1],), jnp.float32, math.log(column_range[0]), math.log(column_range[1])))
    return base_entries * row_scale * column_scale


def projected_draw(key, array_shape):
    entry_key, scale_key = jax.random.split(key)
    base_entries = jax.random.truncated_normal(entry_key, -3.0, 3.0, array_shape, jnp.float32)
    return scaled_block(scale_key, array_shape, base_entries, (1.0, 10.0), (1.0, 10.0))


def draw_image_query(key, part):
    return projected_draw(jax.random.fold_in(key, 11), (BATCH, IMG_TOK, HD)).astype(jnp.bfloat16)


def draw_image_key(key, part):
    return projected_draw(jax.random.fold_in(key, 12), (BATCH, IMG_TOK, HD)).astype(jnp.bfloat16)


def draw_text_key(key, part):
    return projected_draw(jax.random.fold_in(key, 13), (BATCH, TXT_TOK, HD)).astype(jnp.bfloat16)


def draw_position_embed(key, part):
    entry_key, scale_key = jax.random.split(jax.random.fold_in(key, 14))
    array_shape = (REW_TOK, EMB)
    base_entries = jax.random.truncated_normal(entry_key, -3.0, 3.0, array_shape, jnp.float32)
    return scaled_block(scale_key, array_shape, base_entries, (0.03, 0.3), (0.3, 3.0))


def level_of(key, shape, pieces, least, top_value):
    factor_of, own = 1.0, jax.random.fold_in(key, 6)
    for position, parts in pieces:
        draws = jnp.exp(jax.random.uniform(jax.random.fold_in(own, position), (parts,), jnp.float32, least / len(pieces), top_value / len(pieces)))
        factor_of = factor_of * jnp.repeat(draws, shape[position] // parts).reshape([-1 if axis == position else 1 for axis in range(len(shape))])
    return factor_of


def noise(own_key, shape, width, bound, shards=(), held_as=jnp.bfloat16):
    factor_of = level_of(own_key, shape, shards, -0.22, 0.18) if shards else 1.0
    values = jax.random.normal(own_key, shape, jnp.float32) * width * factor_of
    return jnp.minimum(jnp.maximum(values, -bound), bound).astype(held_as)


def setup_inputs(seed: int = 0) -> dict:
    key_of = jax.random.split(jax.random.key(seed), 15)
    image_query = draw_image_query(jax.random.fold_in(key_of[14], 71), 0)
    image_key = draw_image_key(jax.random.fold_in(key_of[14], 71), 0)
    image_value = noise(key_of[2], (BATCH, IMG_TOK, HD), 1.0, 6.0, ((0, 192), (1, 4)))
    text_key = draw_text_key(jax.random.fold_in(key_of[14], 71), 0)
    text_value = noise(key_of[4], (BATCH, TXT_TOK, HD), 1.0, 6.0, ((0, 192), (1, 4)))
    query_gain = jnp.clip(jax.random.uniform(key_of[5], (HEAD,), jnp.float32, 0.6, 1.8), 0.6, 1.8)
    key_gain = jnp.clip(jax.random.uniform(key_of[6], (HEAD,), jnp.float32, 0.6, 1.8), 0.6, 1.8)
    embed_weight = noise(key_of[7], (HD, EMB), HD ** -0.5, 0.15625)
    position_embed = draw_position_embed(jax.random.fold_in(key_of[14], 71), 0)
    norm_gain = jnp.clip(1.0 + 0.15 * jax.random.normal(key_of[9], (EMB,), jnp.float32), 0.25, 1.75)
    final_gain = jnp.clip(1.0 + 0.15 * jax.random.normal(key_of[10], (EMB,), jnp.float32), 0.25, 1.75)
    up_weight = noise(key_of[11], (HID, EMB), EMB ** -0.5, 0.15625, ((0, 768),))
    down_weight = noise(key_of[12], (HID, EMB), HID ** -0.5, 0.109375, ((0, 768),))
    reward_direction = noise(key_of[13], (EMB,), 0.25, 1.5, (), jnp.float32)
    return dict(image_query=image_query, image_key=image_key, image_value=image_value, text_key=text_key, text_value=text_value, query_gain=query_gain, key_gain=key_gain, embed_weight=embed_weight, position_embed=position_embed, norm_gain=norm_gain, final_gain=final_gain, up_weight=up_weight, down_weight=down_weight, reward_direction=reward_direction)


epsilon = 1e-06
root_half = 0.7071067811865476
inv_root_tau = 0.3989422804014327

def norm_heads(features, gain_vector):
    token_count = features.shape[0]
    grouped = features.astype(jnp.float32).reshape(token_count, -1, HEAD)
    inverse_rms = lax.rsqrt(lax.optimization_barrier(jnp.mean(grouped * grouped, axis=-1, keepdims=True)) + epsilon)
    return (grouped * inverse_rms * gain_vector).astype(jnp.bfloat16)

def layer_stats(residual):
    centered = residual - lax.optimization_barrier(jnp.mean(residual, axis=-1, keepdims=True))
    inverse_std = lax.rsqrt(lax.optimization_barrier(jnp.mean(centered * centered, axis=-1, keepdims=True)) + epsilon)
    return (centered * inverse_std, inverse_std)

def layer_back(upstream, normed, inverse_std):
    return inverse_std * (upstream - lax.optimization_barrier(jnp.mean(upstream, axis=-1, keepdims=True)) - normed * lax.optimization_barrier(jnp.mean(upstream * normed, axis=-1, keepdims=True)))

def gelu_parts(preact):
    cumulative = 0.5 * (1.0 + lax.erf(preact * root_half))
    activation = preact * cumulative
    derivative = cumulative + preact * jnp.exp(-0.5 * preact * preact) * inv_root_tau
    return (activation, derivative)

def pool_patches(attended):
    token_count, feature_width = attended.shape
    patch_grid = attended.astype(jnp.float32).reshape(token_count // PATCH_W // 2, 2, PATCH_W // 2, 2, feature_width)
    return lax.optimization_barrier(jnp.mean(patch_grid, axis=(1, 3))).reshape(-1, feature_width).astype(jnp.bfloat16)

def spread_patches(pooled_slope):
    pooled_count, feature_width = pooled_slope.shape
    row_count = pooled_count // (PATCH_W // 2)
    patch_grid = pooled_slope.reshape(row_count, 1, PATCH_W // 2, 1, feature_width)
    patch_grid = jnp.broadcast_to(0.25 * patch_grid, (row_count, 2, PATCH_W // 2, 2, feature_width))
    return patch_grid.reshape(4 * pooled_count, feature_width).astype(jnp.bfloat16)

def group_sum(left_side, right_groups):
    left_groups = left_side.astype(jnp.float32).reshape(left_side.shape[0], N_DP, N_SEQ, -1)
    partials = jnp.einsum('rdsc,dsce->sre', left_groups, right_groups)
    rounded = lax.optimization_barrier(partials.astype(jnp.bfloat16)).astype(jnp.float32)
    return lax.optimization_barrier(jnp.sum(rounded, axis=0))

def reference(image_query, image_key, image_value, text_key, text_value, query_gain, key_gain, embed_weight, position_embed, norm_gain, final_gain, up_weight, down_weight, reward_direction):
    input_groups = up_weight.astype(jnp.float32).reshape(N_DP, N_SEQ, -1, EMB)
    output_groups = down_weight.astype(jnp.float32).reshape(N_DP, N_SEQ, -1, EMB)

    def one_sample(sample):
        query_rows, key_rows, value_rows, text_keys, text_values = sample
        queries = norm_heads(query_rows, query_gain)
        key_heads = norm_heads(jnp.concatenate([text_keys, key_rows], axis=0), key_gain)
        value_heads = jnp.concatenate([text_values, value_rows], axis=0).reshape(-1, HEADS, HEAD)
        scores = jnp.einsum('qhd,khd->hqk', queries.astype(jnp.float32), key_heads.astype(jnp.float32)) * HEAD ** (-0.5)
        exponent = jnp.exp(scores)
        attention_weights = (exponent / lax.optimization_barrier(jnp.sum(exponent, axis=-1, keepdims=True))).astype(jnp.bfloat16)
        mixed_heads = jnp.einsum('hqk,khd->qhd', attention_weights.astype(jnp.float32), value_heads.astype(jnp.float32))
        attended = mixed_heads.astype(jnp.bfloat16).reshape(query_rows.shape[0], HD)
        pooled = pool_patches(attended)
        residual_in = jnp.dot(pooled, embed_weight, preferred_element_type=jnp.float32) + position_embed
        normed_in, inverse_in = layer_stats(residual_in)
        hidden_in = (normed_in * norm_gain).astype(jnp.bfloat16)
        preact = jnp.dot(hidden_in, up_weight.T, preferred_element_type=jnp.float32)
        activation, derivative = gelu_parts(preact)
        branch = group_sum(activation.astype(jnp.bfloat16), output_groups)
        residual_out = residual_in + branch
        normed_out, inverse_out = layer_stats(residual_out)
        direction = final_gain * reward_direction
        reward = jnp.mean(lax.optimization_barrier(jnp.sum(normed_out * direction, axis=-1)))
        out_slope = layer_back(direction, normed_out, inverse_out)
        back_slope = jnp.dot(out_slope.astype(jnp.bfloat16), down_weight.T, preferred_element_type=jnp.float32)
        hidden_slope = (back_slope * derivative).astype(jnp.bfloat16)
        slope_in = group_sum(hidden_slope, input_groups)
        input_slope = out_slope + layer_back(slope_in * norm_gain, normed_in, inverse_in)
        pooled_slope = jnp.dot(input_slope.astype(jnp.bfloat16), embed_weight.T, preferred_element_type=jnp.float32)
        return (attended, spread_patches(pooled_slope), reward)
    outputs = lax.map(one_sample, (image_query, image_key, image_value, text_key, text_value))
    return (outputs[0], outputs[1], outputs[2])
```

```python
import jax
import jax.numpy as jnp
from jax import lax
from jax.experimental import pallas as pl
from jax.experimental.pallas import tpu as pltpu
from jax.sharding import Mesh, PartitionSpec as P


HEAD = 128
IMG, TXT, GROUPS = 64, 128, 4
ROWS = 3 * IMG + 2 * TXT
WIDTH = 384
EMB = 1408
HIDDEN = 768

epsilon = 1e-06
root_half = 0.7071067811865476
inv_root_tau = 0.3989422804014327
f32 = jnp.float32
bf16 = jnp.bfloat16


def pack_body(query, key, value, text_key, text_value, packed):
    for group in range(GROUPS):
        cols = pl.ds(group * WIDTH, WIDTH)
        packed[group, 0:64, :] = query[0, :, cols]
        packed[group, 64:128, :] = key[0, :, cols]
        packed[group, 128:256, :] = text_key[0, :, cols]
        packed[group, 256:320, :] = value[0, :, cols]
        packed[group, 320:448, :] = text_value[0, :, cols]


def norm_rows(rows, gain_row):
    rows = rows.astype(f32)
    inverse_rms = lax.rsqrt(jnp.mean(rows * rows, axis=-1, keepdims=True) + epsilon)
    return (rows * inverse_rms * gain_row).astype(bf16)


def matmul(left_side, right_side):
    return jnp.dot(left_side, right_side, preferred_element_type=f32)


def contract_rows(left_side, right_side):
    return lax.dot_general(left_side, right_side, (((1,), (1,)), ((), ())), preferred_element_type=f32)


def attend_body(packed, query_gain, key_gain, attended, pooled):
    for head in range(3):
        cols = slice(head * HEAD, (head + 1) * HEAD)
        query = jnp.concatenate([packed[s, 0:64, cols] for s in range(GROUPS)], axis=0)
        key = jnp.concatenate([packed[s, 64:256, cols] for s in range(GROUPS)], axis=0)
        value = jnp.concatenate([packed[s, 256:448, cols] for s in range(GROUPS)], axis=0)
        query = norm_rows(query, query_gain[...])
        key = norm_rows(key, key_gain[...])
        exponent = jnp.exp(contract_rows(query, key) * HEAD ** (-0.5))
        total = jnp.sum(exponent, axis=-1, keepdims=True)
        mixed = matmul(exponent.astype(bf16), value) / total
        attended[0, :, cols] = mixed.astype(bf16)
    reward_token = lax.broadcasted_iota(jnp.int32, (64, 256), 0)
    token = lax.broadcasted_iota(jnp.int32, (64, 256), 1)
    same_row = (token >> 6) == (reward_token >> 4)
    same_col = ((token & 31) >> 1) == (reward_token & 15)
    pool = jnp.where(same_row & same_col, 0.25, 0.0).astype(bf16)
    pooled[...] = matmul(pool, attended[0]).astype(bf16)


def layer_stats(residual):
    centered = residual - jnp.mean(residual, axis=-1, keepdims=True)
    inverse_std = lax.rsqrt(jnp.mean(centered * centered, axis=-1, keepdims=True) + epsilon)
    return (centered * inverse_std, inverse_std)


def layer_back(upstream, normed, inverse_std):
    return inverse_std * (
        upstream
        - jnp.mean(upstream, axis=-1, keepdims=True)
        - normed * jnp.mean(upstream * normed, axis=-1, keepdims=True)
    )


def embed_body(pooled, embed_weight, position_embed, residual_in):
    total = position_embed[...]
    for group in range(GROUPS):
        total = total + matmul(pooled[group], embed_weight[group * WIDTH : (group + 1) * WIDTH, :])
    residual_in[...] = total


def by_core(core, first, second, compute):
    @pl.when(core[0] == 0)
    def _():
        compute(first, second)

    @pl.when(core[0] != 0)
    def _():
        compute(second, first)


def forward_body(core, residual_in, norm_gain, first, second, branch, derivative_out, hidden):
    normed, _ = layer_stats(residual_in[...])
    hidden[...] = (normed * norm_gain[...]).astype(bf16)

    def compute(up, down):
        preact = contract_rows(hidden[...], up[...])
        cumulative = 0.5 * (1.0 + lax.erf(preact * root_half))
        derivative_out[...] = cumulative + preact * jnp.exp(-0.5 * preact * preact) * inv_root_tau
        part = matmul((preact * cumulative).astype(bf16), down[...]).astype(bf16)
        for group in range(GROUPS):
            branch[group] = part

    by_core(core, first, second, compute)


def sum_groups(parts):
    total = parts[0].astype(f32)
    for group in range(1, GROUPS):
        total = total + parts[group].astype(f32)
    return total


def backward_body(
    core, residual_in, branch, final_gain, reward_direction, derivative, first, second,
    slope, out_slope_out, reward,
):
    residual_out = residual_in[...] + sum_groups(branch)
    normed, inverse_std = layer_stats(residual_out)
    direction = final_gain[...] * reward_direction[...]
    reward[...] = jnp.full((8, 128), jnp.sum(normed * direction) * (1.0 / 64.0))
    out_slope_out[...] = layer_back(direction, normed, inverse_std)

    def compute(up, down):
        back_slope = contract_rows(out_slope_out[...].astype(bf16), down[...])
        hidden_slope = (back_slope * derivative[...]).astype(bf16)
        part = matmul(hidden_slope, up[...]).astype(bf16)
        for group in range(GROUPS):
            slope[group] = part

    by_core(core, first, second, compute)


def finish_body(group, residual_in, out_slope, slope, norm_gain, embed_weight, gradient):
    embed_rows = embed_weight[pl.ds(pl.multiple_of(group[0] * WIDTH, WIDTH), WIDTH), :]
    normed, inverse_std = layer_stats(residual_in[...])
    weighted = sum_groups(slope) * norm_gain[...]
    input_slope = out_slope[...] + layer_back(weighted, normed, inverse_std)
    pooled_slope = (0.25 * contract_rows(input_slope.astype(bf16), embed_rows)).astype(bf16)
    token = lax.broadcasted_iota(jnp.int32, (256, 64), 0)
    reward_token = lax.broadcasted_iota(jnp.int32, (256, 64), 1)
    same_row = (token >> 6) == (reward_token >> 4)
    same_col = ((token & 31) >> 1) == (reward_token & 15)
    spread = jnp.where(same_row & same_col, 1.0, 0.0).astype(bf16)
    gradient[0] = matmul(spread, pooled_slope).astype(bf16)


def shape(dims, dtype):
    return jax.ShapeDtypeStruct(dims, dtype)


def held(value):
    return pltpu.with_memory_space_constraint(value, pltpu.VMEM)


def in_hbm(value):
    return pltpu.with_memory_space_constraint(value, pltpu.HBM)


def in_vmem(count):
    return [pl.BlockSpec(memory_space=pltpu.VMEM)] * count


scalar_spec = pl.BlockSpec(memory_space=pltpu.SMEM)


def on_device(
    image_query, image_key, image_value, text_key, text_value, query_gain, key_gain, embed_weight,
    position_embed, norm_gain, final_gain, up_weight, down_weight, reward_direction,
):
    core = lax.axis_index("core").astype(jnp.int32).reshape(1)
    group = lax.axis_index("seq").astype(jnp.int32).reshape(1)
    nearby = lax.all_gather(
        jnp.concatenate([up_weight, down_weight], axis=0), ("zl", "core"), axis=0, tiled=False
    )
    nearby_up = nearby[:, 0:4, :].reshape(24, EMB)
    nearby_down = nearby[:, 4:8, :].reshape(24, EMB)
    mine = jnp.where(core[0] == 0, nearby_up, nearby_down)
    mine = lax.all_gather(mine, "x", axis=0, tiled=True)
    first = lax.all_gather(mine, "y", axis=0, tiled=True)
    second = lax.ppermute(first, "core", [(0, 1), (1, 0)])

    first, second = in_hbm(first), in_hbm(second)
    packed = pl.pallas_call(
        pack_body, out_shape=shape((GROUPS, ROWS, WIDTH), bf16), in_specs=in_vmem(5),
        out_specs=pl.BlockSpec(memory_space=pltpu.VMEM), name="pack",
    )(image_query, image_key, image_value, text_key, text_value)
    packed = lax.all_to_all(packed, "seq", split_axis=0, concat_axis=0, tiled=True)
    attended, pooled = pl.pallas_call(
        attend_body, out_shape=(shape((1, 256, WIDTH), bf16), shape((64, WIDTH), bf16)),
        in_specs=in_vmem(3), out_specs=tuple(in_vmem(2)), name="attend",
    )(held(packed), query_gain.reshape(1, HEAD), key_gain.reshape(1, HEAD))
    pooled = lax.all_gather(pooled, "seq", axis=0, tiled=False)
    residual_in = pl.pallas_call(
        embed_body, out_shape=shape((64, EMB), f32), in_specs=in_vmem(3),
        out_specs=pl.BlockSpec(memory_space=pltpu.VMEM), name="embed",
    )(pooled, embed_weight, position_embed)
    gain_row = norm_gain.reshape(1, EMB)
    branch, derivative = pl.pallas_call(
        forward_body, out_shape=(shape((GROUPS, 64, EMB), bf16), shape((64, HIDDEN), f32)),
        in_specs=[scalar_spec, *in_vmem(4)], out_specs=tuple(in_vmem(2)),
        scratch_shapes=[pltpu.VMEM((64, EMB), bf16)], name="forward",
    )(core, residual_in, gain_row, first, second)
    branch = lax.all_to_all(branch, "seq", split_axis=0, concat_axis=0, tiled=True)
    slope, out_slope, reward = pl.pallas_call(
        backward_body,
        out_shape=(shape((GROUPS, 64, EMB), bf16), shape((64, EMB), f32), shape((8, 128), f32)),
        in_specs=[scalar_spec, *in_vmem(7)], out_specs=tuple(in_vmem(3)), name="backward",
    )(
        core, residual_in, held(branch), final_gain.reshape(1, EMB), reward_direction.reshape(1, EMB),
        derivative, first, second,
    )
    slope = lax.all_to_all(slope, "seq", split_axis=0, concat_axis=0, tiled=True)
    gradient = pl.pallas_call(
        finish_body, out_shape=shape((1, 256, WIDTH), bf16),
        in_specs=[scalar_spec, *in_vmem(5)], out_specs=pl.BlockSpec(memory_space=pltpu.VMEM),
        name="finish",
    )(group, residual_in, out_slope, held(slope), gain_row, embed_weight)
    return (attended, gradient, reward[0, 0:1])


def solution(mesh):
    fine = Mesh(mesh.devices.reshape(4, 8, 3, 2, 4), ("x", "y", "zl", "core", "seq"))
    dp = ("x", "y", "zl", "core")
    return jax.shard_map(
        on_device,
        mesh=fine,
        in_specs=(
            P(dp, "seq", None),
            P(dp, "seq", None),
            P(dp, "seq", None),
            P(dp, "seq", None),
            P(dp, "seq", None),
            P(),
            P(),
            P(),
            P(),
            P(),
            P(),
            P((*dp, "seq"), None),
            P((*dp, "seq"), None),
            P(),
        ),
        out_specs=(P(dp, None, "seq"), P(dp, None, "seq"), P(dp)),
        check_vma=False,
    )
```

```python
import jax
import jax.numpy as jnp
from jax import lax
from jax.experimental import pallas as pl
from jax.experimental.pallas import tpu as pltpu
from jax.sharding import Mesh, PartitionSpec as P


HEAD = 128
IMG, TXT, GROUPS = 64, 128, 4
ROWS = 3 * IMG + 2 * TXT
WIDTH = 384
EMB = 1408
HIDDEN = 768


epsilon = 1e-06
root_half = 0.7071067811865476
inv_root_tau = 0.3989422804014327
f32 = jnp.float32
bf16 = jnp.bfloat16


def pack_body(place, query, key, value, text_key, text_value, *packed):
    for step in range(GROUPS):
        group = (place[0] + step) % GROUPS
        cols = pl.ds(pl.multiple_of(group * WIDTH, HEAD), WIDTH)
        packed[step][0:64, :] = query[0, :, cols]
        packed[step][64:128, :] = key[0, :, cols]
        packed[step][128:256, :] = text_key[0, :, cols]
        packed[step][256:320, :] = value[0, :, cols]
        packed[step][320:448, :] = text_value[0, :, cols]


def norm_rows(rows, gain_row):
    rows = rows.astype(f32)
    inverse_rms = lax.rsqrt(jnp.mean(rows * rows, axis=-1, keepdims=True) + epsilon)
    return (rows * inverse_rms * gain_row).astype(bf16)


def matmul(left_side, right_side):
    return jnp.dot(left_side, right_side, preferred_element_type=f32)


def contract_rows(left_side, right_side):
    return lax.dot_general(left_side, right_side, (((1,), (1,)), ((), ())), preferred_element_type=f32)


def attend_body(place, first, second, third, fourth, query_gain, key_gain, attended, pooled):
    packed = (first, second, third, fourth)
    for head in range(3):
        cols = slice(head * HEAD, (head + 1) * HEAD)
        query = jnp.concatenate([packed[s][0:64, cols] for s in range(GROUPS)], axis=0)
        key = jnp.concatenate([packed[s][64:256, cols] for s in range(GROUPS)], axis=0)
        value = jnp.concatenate([packed[s][256:448, cols] for s in range(GROUPS)], axis=0)
        query = norm_rows(query, query_gain[...])
        key = norm_rows(key, key_gain[...])
        exponent = jnp.exp(contract_rows(query, key) * HEAD ** (-0.5))
        total = jnp.sum(exponent, axis=-1, keepdims=True)
        mixed = matmul(exponent.astype(bf16), value) / total
        for step in range(GROUPS):
            source = (place[0] + GROUPS - step) % GROUPS
            rows = pl.ds(pl.multiple_of(source * IMG, IMG), IMG)
            attended[0, rows, cols] = mixed[step * IMG : (step + 1) * IMG].astype(bf16)
    reward_token = lax.broadcasted_iota(jnp.int32, (64, 256), 0)
    token = lax.broadcasted_iota(jnp.int32, (64, 256), 1)
    same_row = (token >> 6) == (reward_token >> 4)
    same_col = ((token & 31) >> 1) == (reward_token & 15)
    pool = jnp.where(same_row & same_col, 0.25, 0.0).astype(bf16)
    pooled[...] = matmul(pool, attended[0]).astype(bf16)


def layer_stats(residual):
    centered = residual - jnp.mean(residual, axis=-1, keepdims=True)
    inverse_std = lax.rsqrt(jnp.mean(centered * centered, axis=-1, keepdims=True) + epsilon)
    return (centered * inverse_std, inverse_std)


def layer_back(upstream, normed, inverse_std):
    return inverse_std * (
        upstream
        - jnp.mean(upstream, axis=-1, keepdims=True)
        - normed * jnp.mean(upstream * normed, axis=-1, keepdims=True)
    )


def embed_body(pooled, embed_weight, position_embed, residual_in):
    total = position_embed[...]
    for group in range(GROUPS):
        total = total + matmul(pooled[group], embed_weight[group * WIDTH : (group + 1) * WIDTH, :])
    residual_in[...] = total


def by_core(core, first, second, compute):
    @pl.when(core[0] == 0)
    def _():
        compute(first, second)

    @pl.when(core[0] != 0)
    def _():
        compute(second, first)


def forward_body(core, residual_in, norm_gain, first, second, branch, derivative_out, hidden):
    normed, _ = layer_stats(residual_in[...])
    hidden[...] = (normed * norm_gain[...]).astype(bf16)

    def compute(up, down):
        preact = contract_rows(hidden[...], up[...])
        cumulative = 0.5 * (1.0 + lax.erf(preact * root_half))
        derivative_out[...] = cumulative + preact * jnp.exp(-0.5 * preact * preact) * inv_root_tau
        part = matmul((preact * cumulative).astype(bf16), down[...]).astype(bf16)
        for group in range(GROUPS):
            branch[group] = part

    by_core(core, first, second, compute)


def sum_groups(parts):
    total = parts[0].astype(f32)
    for group in range(1, GROUPS):
        total = total + parts[group].astype(f32)
    return total


def backward_body(
    core, residual_in, branch, final_gain, reward_direction, derivative, first, second,
    slope, out_slope_out, reward,
):
    residual_out = residual_in[...] + sum_groups(branch)
    normed, inverse_std = layer_stats(residual_out)
    direction = final_gain[...] * reward_direction[...]
    reward[...] = jnp.full((8, 128), jnp.sum(normed * direction) * (1.0 / 64.0))
    out_slope_out[...] = layer_back(direction, normed, inverse_std)

    def compute(up, down):
        back_slope = contract_rows(out_slope_out[...].astype(bf16), down[...])
        hidden_slope = (back_slope * derivative[...]).astype(bf16)
        part = matmul(hidden_slope, up[...]).astype(bf16)
        for group in range(GROUPS):
            slope[group] = part

    by_core(core, first, second, compute)


def finish_body(group, residual_in, out_slope, slope, norm_gain, embed_weight, gradient):
    embed_rows = embed_weight[pl.ds(pl.multiple_of(group[0] * WIDTH, WIDTH), WIDTH), :]
    normed, inverse_std = layer_stats(residual_in[...])
    weighted = sum_groups(slope) * norm_gain[...]
    input_slope = out_slope[...] + layer_back(weighted, normed, inverse_std)
    pooled_slope = (0.25 * contract_rows(input_slope.astype(bf16), embed_rows)).astype(bf16)
    token = lax.broadcasted_iota(jnp.int32, (256, 64), 0)
    reward_token = lax.broadcasted_iota(jnp.int32, (256, 64), 1)
    same_row = (token >> 6) == (reward_token >> 4)
    same_col = ((token & 31) >> 1) == (reward_token & 15)
    spread = jnp.where(same_row & same_col, 1.0, 0.0).astype(bf16)
    gradient[0] = matmul(spread, pooled_slope).astype(bf16)


def shape(dims, dtype):
    return jax.ShapeDtypeStruct(dims, dtype)


def held(value):
    return pltpu.with_memory_space_constraint(value, pltpu.VMEM)


def in_hbm(value):
    return pltpu.with_memory_space_constraint(value, pltpu.HBM)


def in_vmem(count):
    return [pl.BlockSpec(memory_space=pltpu.VMEM)] * count


scalar_spec = pl.BlockSpec(memory_space=pltpu.SMEM)


def spread_to(value, axes, count):
    copies = jnp.broadcast_to(value[None], (count, *value.shape))
    return lax.all_to_all(copies, axes, split_axis=0, concat_axis=0, tiled=True)


def on_device(
    image_query, image_key, image_value, text_key, text_value, query_gain, key_gain, embed_weight,
    position_embed, norm_gain, final_gain, up_weight, down_weight, reward_direction,
):
    core = lax.axis_index("core").astype(jnp.int32).reshape(1)
    group = lax.axis_index("seq").astype(jnp.int32).reshape(1)
    nearby = spread_to(jnp.concatenate([up_weight, down_weight], axis=0), ("zl", "core"), 6)
    nearby_up = nearby[:, 0:4, :].reshape(24, EMB)
    nearby_down = nearby[:, 4:8, :].reshape(24, EMB)
    mine = jnp.where(core[0] == 0, nearby_up, nearby_down)
    mine = lax.all_gather(mine, "x", axis=0, tiled=True)
    first = spread_to(mine, "y", 8).reshape(HIDDEN, EMB)
    second = lax.ppermute(first, "core", [(0, 1), (1, 0)])

    first, second = in_hbm(first), in_hbm(second)
    packed = pl.pallas_call(
        pack_body, out_shape=(shape((ROWS, WIDTH), bf16),) * GROUPS, in_specs=[scalar_spec, *in_vmem(5)],
        out_specs=tuple(in_vmem(GROUPS)), name="pack",
    )(group, image_query, image_key, image_value, text_key, text_value)
    received = [packed[0]]
    for step in (2, 1, 3):
        around = [(member, (member + step) % GROUPS) for member in range(GROUPS)]
        received.append(lax.ppermute(packed[step], "seq", around))
    received = [received[0], received[2], received[1], received[3]]
    attended, pooled = pl.pallas_call(
        attend_body, out_shape=(shape((1, 256, WIDTH), bf16), shape((64, WIDTH), bf16)),
        in_specs=[scalar_spec, *in_vmem(6)], out_specs=tuple(in_vmem(2)), name="attend",
    )(group, *map(held, received), query_gain.reshape(1, HEAD), key_gain.reshape(1, HEAD))
    pooled = lax.all_gather(pooled, "seq", axis=0, tiled=False)
    residual_in = pl.pallas_call(
        embed_body, out_shape=shape((64, EMB), f32), in_specs=in_vmem(3),
        out_specs=pl.BlockSpec(memory_space=pltpu.VMEM), name="embed",
    )(pooled, embed_weight, position_embed)
    gain_row = norm_gain.reshape(1, EMB)
    branch, derivative = pl.pallas_call(
        forward_body, out_shape=(shape((GROUPS, 64, EMB), bf16), shape((64, HIDDEN), f32)),
        in_specs=[scalar_spec, *in_vmem(4)], out_specs=tuple(in_vmem(2)),
        scratch_shapes=[pltpu.VMEM((64, EMB), bf16)], name="forward",
    )(core, residual_in, gain_row, first, second)
    branch = lax.all_to_all(branch, "seq", split_axis=0, concat_axis=0, tiled=True)
    slope, out_slope, reward = pl.pallas_call(
        backward_body,
        out_shape=(shape((GROUPS, 64, EMB), bf16), shape((64, EMB), f32), shape((8, 128), f32)),
        in_specs=[scalar_spec, *in_vmem(7)], out_specs=tuple(in_vmem(3)), name="backward",
    )(
        core, residual_in, held(branch), final_gain.reshape(1, EMB), reward_direction.reshape(1, EMB),
        derivative, first, second,
    )
    slope = lax.all_to_all(slope, "seq", split_axis=0, concat_axis=0, tiled=True)
    gradient = pl.pallas_call(
        finish_body, out_shape=shape((1, 256, WIDTH), bf16),
        in_specs=[scalar_spec, *in_vmem(5)], out_specs=pl.BlockSpec(memory_space=pltpu.VMEM),
        name="finish",
    )(group, residual_in, out_slope, held(slope), gain_row, embed_weight)
    return (attended, gradient, reward[0, 0:1])


def solution(mesh):
    fine = Mesh(mesh.devices.reshape(4, 8, 3, 2, 4), ("x", "y", "zl", "core", "seq"))
    dp = ("x", "y", "zl", "core")
    return jax.shard_map(
        on_device,
        mesh=fine,
        in_specs=(
            P(dp, "seq", None),
            P(dp, "seq", None),
            P(dp, "seq", None),
            P(dp, "seq", None),
            P(dp, "seq", None),
            P(),
            P(),
            P(),
            P(),
            P(),
            P(),
            P((*dp, "seq"), None),
            P((*dp, "seq"), None),
            P(),
        ),
        out_specs=(P(dp, None, "seq"), P(dp, None, "seq"), P(dp)),
        check_vma=False,
    )
```

```python
import jax
import jax.numpy as jnp
from jax import lax
from jax.experimental import pallas as pl
from jax.experimental.pallas import tpu as pltpu
from jax.sharding import Mesh, PartitionSpec as P


HEAD = 128
IMG, TXT, GROUPS = 64, 128, 4
ROWS = 3 * IMG + 2 * TXT
WIDTH = 384
EMB = 1408
HIDDEN = 768


epsilon = 1e-06
root_half = 0.7071067811865476
inv_root_tau = 0.3989422804014327
f32 = jnp.float32
bf16 = jnp.bfloat16


def pack_body(place, query, key, value, text_key, text_value, *packed):
    for step in range(GROUPS):
        group = (place[0] + step) % GROUPS
        cols = pl.ds(pl.multiple_of(group * WIDTH, HEAD), WIDTH)
        packed[step][0:64, :] = query[0, :, cols]
        packed[step][64:128, :] = key[0, :, cols]
        packed[step][128:256, :] = text_key[0, :, cols]
        packed[step][256:320, :] = value[0, :, cols]
        packed[step][320:448, :] = text_value[0, :, cols]


def norm_rows(rows, gain_row):
    rows = rows.astype(f32)
    inverse_rms = lax.rsqrt(jnp.mean(rows * rows, axis=-1, keepdims=True) + epsilon)
    return (rows * inverse_rms * gain_row).astype(bf16)


def matmul(left_side, right_side):
    return jnp.dot(left_side, right_side, preferred_element_type=f32)


def contract_rows(left_side, right_side):
    return lax.dot_general(left_side, right_side, (((1,), (1,)), ((), ())), preferred_element_type=f32)


def attend_body(place, first, second, third, fourth, query_gain, key_gain, attended, pooled):
    packed = (first, second, third, fourth)
    for head in range(3):
        cols = slice(head * HEAD, (head + 1) * HEAD)
        query = jnp.concatenate([packed[s][0:64, cols] for s in range(GROUPS)], axis=0)
        key = jnp.concatenate([packed[s][64:256, cols] for s in range(GROUPS)], axis=0)
        value = jnp.concatenate([packed[s][256:448, cols] for s in range(GROUPS)], axis=0)
        query = norm_rows(query, query_gain[...])
        key = norm_rows(key, key_gain[...])
        exponent = jnp.exp(contract_rows(query, key) * HEAD ** (-0.5))
        total = jnp.sum(exponent, axis=-1, keepdims=True)
        mixed = matmul(exponent.astype(bf16), value) / total
        for step in range(GROUPS):
            source = (place[0] + GROUPS - step) % GROUPS
            rows = pl.ds(pl.multiple_of(source * IMG, IMG), IMG)
            attended[0, rows, cols] = mixed[step * IMG : (step + 1) * IMG].astype(bf16)
    reward_token = lax.broadcasted_iota(jnp.int32, (64, 256), 0)
    token = lax.broadcasted_iota(jnp.int32, (64, 256), 1)
    same_row = (token >> 6) == (reward_token >> 4)
    same_col = ((token & 31) >> 1) == (reward_token & 15)
    pool = jnp.where(same_row & same_col, 0.25, 0.0).astype(bf16)
    pooled[...] = matmul(pool, attended[0]).astype(bf16)


def layer_stats(residual):
    centered = residual - jnp.mean(residual, axis=-1, keepdims=True)
    inverse_std = lax.rsqrt(jnp.mean(centered * centered, axis=-1, keepdims=True) + epsilon)
    return (centered * inverse_std, inverse_std)


def layer_back(upstream, normed, inverse_std):
    return inverse_std * (
        upstream
        - jnp.mean(upstream, axis=-1, keepdims=True)
        - normed * jnp.mean(upstream * normed, axis=-1, keepdims=True)
    )


def embed_body(pooled, embed_weight, position_embed, residual_in):
    total = position_embed[...]
    for group in range(GROUPS):
        total = total + matmul(pooled[group], embed_weight[group * WIDTH : (group + 1) * WIDTH, :])
    residual_in[...] = total


def by_core(core, first, second, compute):
    @pl.when(core[0] == 0)
    def _():
        compute(first, second)

    @pl.when(core[0] != 0)
    def _():
        compute(second, first)


def forward_body(core, residual_in, norm_gain, first, second, low, high, derivative_out, hidden):
    normed, _ = layer_stats(residual_in[...])
    hidden[...] = (normed * norm_gain[...]).astype(bf16)

    def compute(up, down):
        preact = contract_rows(hidden[...], up[...])
        cumulative = 0.5 * (1.0 + lax.erf(preact * root_half))
        derivative_out[...] = cumulative + preact * jnp.exp(-0.5 * preact * preact) * inv_root_tau
        part = matmul((preact * cumulative).astype(bf16), down[...]).astype(bf16)
        low[...] = part[0:32]
        high[...] = part[32:64]

    by_core(core, first, second, compute)


def sum_halves(halves):
    low, low_other, high, high_other = halves
    low = low[...].astype(f32) + low_other[...].astype(f32)
    high = high[...].astype(f32) + high_other[...].astype(f32)
    return jnp.concatenate([low, high], axis=0)


def group_sum(low, high):
    inner = [(0, 1), (1, 0), (2, 3), (3, 2)]
    outer = [(0, 3), (3, 0), (1, 2), (2, 1)]

    def pair_sum(mine, other):
        return (mine.astype(f32) + other.astype(f32)).astype(bf16)

    low_pair = lax.ppermute(low, "seq", inner)
    high_pair = lax.ppermute(high, "seq", outer)
    low, high = pair_sum(low, low_pair), pair_sum(high, high_pair)
    return (low, lax.ppermute(low, "seq", outer), high, lax.ppermute(high, "seq", inner))


def backward_body(
    core, residual_in, b0, b1, b2, b3, final_gain, reward_direction, derivative, first, second,
    low, high, out_slope_out, reward,
):
    residual_out = residual_in[...] + sum_halves((b0, b1, b2, b3))
    normed, inverse_std = layer_stats(residual_out)
    direction = final_gain[...] * reward_direction[...]
    reward[...] = jnp.full((8, 128), jnp.sum(normed * direction) * (1.0 / 64.0))
    out_slope_out[...] = layer_back(direction, normed, inverse_std)

    def compute(up, down):
        back_slope = contract_rows(out_slope_out[...].astype(bf16), down[...])
        hidden_slope = (back_slope * derivative[...]).astype(bf16)
        part = matmul(hidden_slope, up[...]).astype(bf16)
        low[...] = part[0:32]
        high[...] = part[32:64]

    by_core(core, first, second, compute)


def finish_body(group, residual_in, out_slope, s0, s1, s2, s3, norm_gain, embed_weight, gradient):
    embed_rows = embed_weight[pl.ds(pl.multiple_of(group[0] * WIDTH, WIDTH), WIDTH), :]
    normed, inverse_std = layer_stats(residual_in[...])
    weighted = sum_halves((s0, s1, s2, s3)) * norm_gain[...]
    input_slope = out_slope[...] + layer_back(weighted, normed, inverse_std)
    pooled_slope = (0.25 * contract_rows(input_slope.astype(bf16), embed_rows)).astype(bf16)
    token = lax.broadcasted_iota(jnp.int32, (256, 64), 0)
    reward_token = lax.broadcasted_iota(jnp.int32, (256, 64), 1)
    same_row = (token >> 6) == (reward_token >> 4)
    same_col = ((token & 31) >> 1) == (reward_token & 15)
    spread = jnp.where(same_row & same_col, 1.0, 0.0).astype(bf16)
    gradient[0] = matmul(spread, pooled_slope).astype(bf16)


def shape(dims, dtype):
    return jax.ShapeDtypeStruct(dims, dtype)


def held(value):
    return pltpu.with_memory_space_constraint(value, pltpu.VMEM)


def in_hbm(value):
    return pltpu.with_memory_space_constraint(value, pltpu.HBM)


def in_vmem(count):
    return [pl.BlockSpec(memory_space=pltpu.VMEM)] * count


scalar_spec = pl.BlockSpec(memory_space=pltpu.SMEM)


def spread_to(value, axes, count):
    copies = jnp.broadcast_to(value[None], (count, *value.shape))
    return lax.all_to_all(copies, axes, split_axis=0, concat_axis=0, tiled=True)


def on_device(
    image_query, image_key, image_value, text_key, text_value, query_gain, key_gain, embed_weight,
    position_embed, norm_gain, final_gain, up_weight, down_weight, reward_direction,
):
    core = lax.axis_index("core").astype(jnp.int32).reshape(1)
    group = lax.axis_index("seq").astype(jnp.int32).reshape(1)
    nearby = spread_to(jnp.concatenate([up_weight, down_weight], axis=0), ("zl", "core"), 6)
    nearby_up = nearby[:, 0:4, :].reshape(24, EMB)
    nearby_down = nearby[:, 4:8, :].reshape(24, EMB)
    mine = jnp.where(core[0] == 0, nearby_up, nearby_down)
    mine = spread_to(mine, "y", 8).reshape(192, EMB)
    first = spread_to(mine, "x", 4).reshape(HIDDEN, EMB)
    second = lax.ppermute(first, "core", [(0, 1), (1, 0)])

    first = in_hbm(first)
    packed = pl.pallas_call(
        pack_body, out_shape=(shape((ROWS, WIDTH), bf16),) * GROUPS, in_specs=[scalar_spec, *in_vmem(5)],
        out_specs=tuple(in_vmem(GROUPS)), name="pack",
    )(group, image_query, image_key, image_value, text_key, text_value)
    received = [packed[0]]
    for step in (2, 1, 3):
        around = [(member, (member + step) % GROUPS) for member in range(GROUPS)]
        received.append(lax.ppermute(packed[step], "seq", around))
    received = [received[0], received[2], received[1], received[3]]
    attended, pooled = pl.pallas_call(
        attend_body, out_shape=(shape((1, 256, WIDTH), bf16), shape((64, WIDTH), bf16)),
        in_specs=[scalar_spec, *in_vmem(6)], out_specs=tuple(in_vmem(2)), name="attend",
    )(group, *map(held, received), query_gain.reshape(1, HEAD), key_gain.reshape(1, HEAD))
    pooled = lax.all_gather(pooled, "seq", axis=0, tiled=False)
    residual_in = pl.pallas_call(
        embed_body, out_shape=shape((64, EMB), f32), in_specs=in_vmem(3),
        out_specs=pl.BlockSpec(memory_space=pltpu.VMEM), name="embed",
    )(pooled, embed_weight, position_embed)
    gain_row = norm_gain.reshape(1, EMB)
    half = shape((32, EMB), bf16)
    low, high, derivative = pl.pallas_call(
        forward_body, out_shape=(half, half, shape((64, HIDDEN), f32)),
        in_specs=[scalar_spec, *in_vmem(4)], out_specs=tuple(in_vmem(3)),
        scratch_shapes=[pltpu.VMEM((64, EMB), bf16)], name="forward",
    )(core, residual_in, gain_row, first, held(second))
    branch = group_sum(low, high)
    low, high, out_slope, reward = pl.pallas_call(
        backward_body, out_shape=(half, half, shape((64, EMB), f32), shape((8, 128), f32)),
        in_specs=[scalar_spec, *in_vmem(10)], out_specs=tuple(in_vmem(4)), name="backward",
    )(
        core, residual_in, *map(held, branch), final_gain.reshape(1, EMB), reward_direction.reshape(1, EMB),
        derivative, first, in_hbm(second),
    )
    slope = group_sum(low, high)
    gradient = pl.pallas_call(
        finish_body, out_shape=shape((1, 256, WIDTH), bf16), in_specs=[scalar_spec, *in_vmem(8)],
        out_specs=pl.BlockSpec(memory_space=pltpu.VMEM), name="finish",
    )(group, residual_in, out_slope, *map(held, slope), gain_row, embed_weight)
    return (attended, gradient, reward[0, 0:1])


def solution(mesh):
    fine = Mesh(mesh.devices.reshape(4, 8, 3, 2, 4), ("x", "y", "zl", "core", "seq"))
    dp = ("x", "y", "zl", "core")
    return jax.shard_map(
        on_device,
        mesh=fine,
        in_specs=(
            P(dp, "seq", None),
            P(dp, "seq", None),
            P(dp, "seq", None),
            P(dp, "seq", None),
            P(dp, "seq", None),
            P(),
            P(),
            P(),
            P(),
            P(),
            P(),
            P((*dp, "seq"), None),
            P((*dp, "seq"), None),
            P(),
        ),
        out_specs=(P(dp, None, "seq"), P(dp, None, "seq"), P(dp)),
        check_vma=False,
    )
```

```python
import jax
import jax.numpy as jnp
from jax import lax
from jax.experimental import pallas as pl
from jax.experimental.pallas import tpu as pltpu
from jax.sharding import Mesh, PartitionSpec as P


HEAD = 128
IMG, TXT, GROUPS = 64, 128, 4
ROWS = 3 * IMG + 2 * TXT
WIDTH = 384
EMB = 1408
HIDDEN = 768


epsilon = 1e-06
root_half = 0.7071067811865476
inv_root_tau = 0.3989422804014327
f32 = jnp.float32
bf16 = jnp.bfloat16


def pack_body(
    place, query, key, value, text_key, text_value, norm_gain, final_gain, reward_direction, up, down,
    p0, p1, p2, p3, gain_row, direction_row, copies,
):
    rows = jnp.concatenate([up[...], down[...]], axis=0)
    for member in range(6):
        copies[member] = rows
    gain_row[...] = norm_gain[...].reshape(1, EMB)
    direction_row[...] = (final_gain[...] * reward_direction[...]).reshape(1, EMB)
    packed = (p0, p1, p2, p3)
    for step in range(GROUPS):
        group = (place[0] + step) % GROUPS
        cols = pl.ds(pl.multiple_of(group * WIDTH, HEAD), WIDTH)
        packed[step][0:64, :] = query[0, :, cols]
        packed[step][64:128, :] = key[0, :, cols]
        packed[step][128:256, :] = text_key[0, :, cols]
        packed[step][256:320, :] = value[0, :, cols]
        packed[step][320:448, :] = text_value[0, :, cols]


def norm_rows(rows, gain_row):
    rows = rows.astype(f32)
    inverse_rms = lax.rsqrt(jnp.mean(rows * rows, axis=-1, keepdims=True) + epsilon)
    return (rows * inverse_rms * gain_row).astype(bf16)


def matmul(left_side, right_side):
    return jnp.dot(left_side, right_side, preferred_element_type=f32)


def contract_rows(left_side, right_side):
    return lax.dot_general(left_side, right_side, (((1,), (1,)), ((), ())), preferred_element_type=f32)


def attend_body(place, first, second, third, fourth, query_gain, key_gain, attended, pooled):
    packed = (first, second, third, fourth)
    for head in range(3):
        cols = slice(head * HEAD, (head + 1) * HEAD)
        query = jnp.concatenate([packed[s][0:64, cols] for s in range(GROUPS)], axis=0)
        key = jnp.concatenate([packed[s][64:256, cols] for s in range(GROUPS)], axis=0)
        value = jnp.concatenate([packed[s][256:448, cols] for s in range(GROUPS)], axis=0)
        query = norm_rows(query, query_gain[...])
        key = norm_rows(key, key_gain[...])
        exponent = jnp.exp(contract_rows(query, key) * HEAD ** (-0.5))
        total = jnp.sum(exponent, axis=-1, keepdims=True)
        mixed = matmul(exponent.astype(bf16), value) / total
        for step in range(GROUPS):
            source = (place[0] + GROUPS - step) % GROUPS
            rows = pl.ds(pl.multiple_of(source * IMG, IMG), IMG)
            attended[0, rows, cols] = mixed[step * IMG : (step + 1) * IMG].astype(bf16)
    reward_token = lax.broadcasted_iota(jnp.int32, (64, 256), 0)
    token = lax.broadcasted_iota(jnp.int32, (64, 256), 1)
    same_row = (token >> 6) == (reward_token >> 4)
    same_col = ((token & 31) >> 1) == (reward_token & 15)
    pool = jnp.where(same_row & same_col, 0.25, 0.0).astype(bf16)
    pooled[...] = matmul(pool, attended[0]).astype(bf16)


def layer_stats(residual):
    centered = residual - jnp.mean(residual, axis=-1, keepdims=True)
    inverse_std = lax.rsqrt(jnp.mean(centered * centered, axis=-1, keepdims=True) + epsilon)
    return (centered * inverse_std, inverse_std)


def layer_back(upstream, normed, inverse_std):
    return inverse_std * (
        upstream
        - jnp.mean(upstream, axis=-1, keepdims=True)
        - normed * jnp.mean(upstream * normed, axis=-1, keepdims=True)
    )


def embed_body(pooled, embed_weight, position_embed, residual_in, weight, sems):
    def part(group):
        rows = pl.ds(group * WIDTH, WIDTH)
        return pltpu.make_async_copy(embed_weight.at[rows, :], weight.at[rows, :], sems.at[group])

    for group in range(GROUPS):
        part(group).start()
    total = position_embed[...]
    for group in range(GROUPS):
        part(group).wait()
        total = total + matmul(pooled[group], weight[group * WIDTH : (group + 1) * WIDTH, :])
    residual_in[...] = total


def by_core(core, first, second, compute):
    @pl.when(core[0] == 0)
    def _():
        compute(first, second)

    @pl.when(core[0] != 0)
    def _():
        compute(second, first)


def forward_body(core, residual_in, norm_gain, first_rows, second, low, high, derivative_out, hidden, first, sem):
    fetch = pltpu.make_async_copy(first_rows, first, sem)
    fetch.start()
    normed, _ = layer_stats(residual_in[...])
    hidden[...] = (normed * norm_gain[...]).astype(bf16)
    fetch.wait()

    def compute(up, down):
        preact = contract_rows(hidden[...], up[...])
        cumulative = 0.5 * (1.0 + lax.erf(preact * root_half))
        derivative_out[...] = cumulative + preact * jnp.exp(-0.5 * preact * preact) * inv_root_tau
        part = matmul((preact * cumulative).astype(bf16), down[...]).astype(bf16)
        low[...] = part[0:32]
        high[...] = part[32:64]

    by_core(core, first, second, compute)


def sum_halves(halves):
    low, low_other, high, high_other = halves
    low = low[...].astype(f32) + low_other[...].astype(f32)
    high = high[...].astype(f32) + high_other[...].astype(f32)
    return jnp.concatenate([low, high], axis=0)


def group_sum(low, high):
    inner = [(0, 1), (1, 0), (2, 3), (3, 2)]
    outer = [(0, 3), (3, 0), (1, 2), (2, 1)]

    def pair_sum(mine, other):
        return (mine.astype(f32) + other.astype(f32)).astype(bf16)

    low_pair = lax.ppermute(low, "seq", inner)
    high_pair = lax.ppermute(high, "seq", outer)
    low, high = pair_sum(low, low_pair), pair_sum(high, high_pair)
    return (low, lax.ppermute(low, "seq", outer), high, lax.ppermute(high, "seq", inner))


def backward_body(
    core, residual_in, b0, b1, b2, b3, norm_gain, direction_row, derivative, first_rows, second_rows, embed_rows,
    blocks, reward, out_slope, part, first, second, embed_weight, sems,
):
    copies = [
        pltpu.make_async_copy(first_rows, first, sems.at[0]),
        pltpu.make_async_copy(second_rows, second, sems.at[1]),
        pltpu.make_async_copy(embed_rows, embed_weight, sems.at[2]),
    ]
    for copy in copies:
        copy.start()
    residual_out = residual_in[...] + sum_halves((b0, b1, b2, b3))
    normed, inverse_std = layer_stats(residual_out)
    direction = direction_row[...]
    reward[0] = jnp.sum(normed * direction) * (1.0 / 64.0)
    out_slope[...] = layer_back(direction, normed, inverse_std)
    copies[0].wait()
    copies[1].wait()

    def compute(up, down):
        back_slope = contract_rows(out_slope[...].astype(bf16), down[...])
        hidden_slope = (back_slope * derivative[...]).astype(bf16)
        part[...] = matmul(hidden_slope, up[...])

    by_core(core, first, second, compute)
    normed, inverse_std = layer_stats(residual_in[...])
    share = layer_back(part[...] * norm_gain[...], normed, inverse_std)
    share = (share + 0.25 * out_slope[...]).astype(bf16)
    copies[2].wait()
    for group in range(GROUPS):
        rows = slice(group * WIDTH, (group + 1) * WIDTH)
        blocks[group] = (0.25 * contract_rows(share, embed_weight[rows, :])).astype(bf16)


def finish_body(blocks, gradient):
    pooled_slope = blocks[0].astype(f32)
    for group in range(1, GROUPS):
        pooled_slope = pooled_slope + blocks[group].astype(f32)
    token = lax.broadcasted_iota(jnp.int32, (256, 64), 0)
    reward_token = lax.broadcasted_iota(jnp.int32, (256, 64), 1)
    same_row = (token >> 6) == (reward_token >> 4)
    same_col = ((token & 31) >> 1) == (reward_token & 15)
    spread = jnp.where(same_row & same_col, 1.0, 0.0).astype(bf16)
    gradient[0] = matmul(spread, pooled_slope.astype(bf16)).astype(bf16)


def shape(dims, dtype):
    return jax.ShapeDtypeStruct(dims, dtype)


def held(value):
    return pltpu.with_memory_space_constraint(value, pltpu.VMEM)


def in_any(count):
    return [pl.BlockSpec(memory_space=pl.ANY)] * count


def in_hbm(value):
    return pltpu.with_memory_space_constraint(value, pltpu.HBM)


def in_vmem(count):
    return [pl.BlockSpec(memory_space=pltpu.VMEM)] * count


scalar_spec = pl.BlockSpec(memory_space=pltpu.SMEM)


def spread_to(value, axes, count):
    copies = jnp.broadcast_to(value[None], (count, *value.shape))
    return lax.all_to_all(copies, axes, split_axis=0, concat_axis=0, tiled=True)


def on_device(
    image_query, image_key, image_value, text_key, text_value, query_gain, key_gain, embed_weight,
    position_embed, norm_gain, final_gain, up_weight, down_weight, reward_direction,
):
    core = lax.axis_index("core").astype(jnp.int32).reshape(1)
    group = lax.axis_index("seq").astype(jnp.int32).reshape(1)
    packed = pl.pallas_call(
        pack_body,
        out_shape=(
            *(shape((ROWS, WIDTH), bf16),) * GROUPS, shape((1, EMB), f32), shape((1, EMB), f32),
            shape((6, 8, EMB), bf16),
        ),
        in_specs=[scalar_spec, *in_vmem(10)], out_specs=tuple(in_vmem(7)), name="pack",
    )(
        group, image_query, image_key, image_value, text_key, text_value, norm_gain, final_gain,
        reward_direction, up_weight, down_weight,
    )
    *packed, gain_row, direction_row, copies = packed
    nearby = lax.all_to_all(copies, ("zl", "core"), split_axis=0, concat_axis=0, tiled=True)
    nearby_up = nearby[:, 0:4, :].reshape(24, EMB)
    nearby_down = nearby[:, 4:8, :].reshape(24, EMB)
    mine = jnp.where(core[0] == 0, nearby_up, nearby_down)
    mine = spread_to(mine, "y", 8).reshape(192, EMB)
    first = spread_to(mine, "x", 4).reshape(HIDDEN, EMB)
    second = lax.ppermute(first, "core", [(0, 1), (1, 0)])

    first = in_hbm(first)
    received = [packed[0]]
    for step in (2, 1, 3):
        around = [(member, (member + step) % GROUPS) for member in range(GROUPS)]
        received.append(lax.ppermute(packed[step], "seq", around))
    received = [received[0], received[2], received[1], received[3]]
    attended, pooled = pl.pallas_call(
        attend_body, out_shape=(shape((1, 256, WIDTH), bf16), shape((64, WIDTH), bf16)),
        in_specs=[scalar_spec, *in_vmem(6)], out_specs=tuple(in_vmem(2)), name="attend",
    )(group, *map(held, received), query_gain.reshape(1, HEAD), key_gain.reshape(1, HEAD))
    pooled = lax.all_gather(pooled, "seq", axis=0, tiled=False)
    residual_in = pl.pallas_call(
        embed_body, out_shape=shape((64, EMB), f32),
        in_specs=[in_vmem(1)[0], *in_any(1), *in_vmem(1)], out_specs=pl.BlockSpec(memory_space=pltpu.VMEM),
        scratch_shapes=[pltpu.VMEM((1536, EMB), bf16), pltpu.SemaphoreType.DMA((GROUPS,))], name="embed",
    )(pooled, embed_weight, position_embed)
    half = shape((32, EMB), bf16)
    low, high, derivative = pl.pallas_call(
        forward_body, out_shape=(half, half, shape((64, HIDDEN), f32)),
        in_specs=[scalar_spec, *in_vmem(2), *in_any(1), *in_vmem(1)], out_specs=tuple(in_vmem(3)),
        scratch_shapes=[
            pltpu.VMEM((64, EMB), bf16), pltpu.VMEM((HIDDEN, EMB), bf16), pltpu.SemaphoreType.DMA,
        ],
        name="forward",
    )(core, residual_in, gain_row, first, held(second))
    branch = group_sum(low, high)
    blocks, reward = pl.pallas_call(
        backward_body, out_shape=(shape((GROUPS, 64, WIDTH), bf16), shape((1,), f32)),
        in_specs=[scalar_spec, *in_vmem(8), *in_any(3)], out_specs=(in_vmem(1)[0], scalar_spec),
        scratch_shapes=[
            pltpu.VMEM((64, EMB), f32), pltpu.VMEM((64, EMB), f32), pltpu.VMEM((HIDDEN, EMB), bf16),
            pltpu.VMEM((HIDDEN, EMB), bf16), pltpu.VMEM((1536, EMB), bf16), pltpu.SemaphoreType.DMA((3,)),
        ],
        name="backward",
    )(
        core, residual_in, *map(held, branch), gain_row, direction_row, derivative, first, in_hbm(second),
        embed_weight,
    )
    blocks = lax.all_to_all(blocks, "seq", split_axis=0, concat_axis=0, tiled=True)
    gradient = pl.pallas_call(
        finish_body, out_shape=shape((1, 256, WIDTH), bf16), in_specs=in_vmem(1),
        out_specs=pl.BlockSpec(memory_space=pltpu.VMEM), name="finish",
    )(held(blocks))
    return (attended, gradient, reward)


def solution(mesh):
    fine = Mesh(mesh.devices.reshape(4, 8, 3, 2, 4), ("x", "y", "zl", "core", "seq"))
    dp = ("x", "y", "zl", "core")
    return jax.shard_map(
        on_device,
        mesh=fine,
        in_specs=(
            P(dp, "seq", None),
            P(dp, "seq", None),
            P(dp, "seq", None),
            P(dp, "seq", None),
            P(dp, "seq", None),
            P(),
            P(),
            P(),
            P(),
            P(),
            P(),
            P((*dp, "seq"), None),
            P((*dp, "seq"), None),
            P(),
        ),
        out_specs=(P(dp, None, "seq"), P(dp, None, "seq"), P(dp)),
        check_vma=False,
    )
```

```python
import jax
import jax.numpy as jnp
from jax import lax
from jax.experimental import pallas as pl
from jax.experimental.pallas import tpu as pltpu
from jax.sharding import Mesh, PartitionSpec as P


HEAD = 128
IMG, TXT, GROUPS = 64, 128, 4
ROWS = 3 * IMG + 2 * TXT
WIDTH = 384
EMB = 1408
HIDDEN = 768


epsilon = 1e-06
root_half = 0.7071067811865476
inv_root_tau = 0.3989422804014327
f32 = jnp.float32
bf16 = jnp.bfloat16


def pack_body(
    place, query, key, value, text_key, text_value, norm_gain, final_gain, reward_direction, up, down,
    p0, p1, p2, p3, gain_row, direction_row, copies,
):
    rows = jnp.concatenate([up[...], down[...]], axis=0)
    for member in range(6):
        copies[member] = rows
    gain_row[...] = norm_gain[...].reshape(1, EMB)
    direction_row[...] = (final_gain[...] * reward_direction[...]).reshape(1, EMB)
    packed = (p0, p1, p2, p3)
    for step in range(GROUPS):
        group = (place[0] + step) % GROUPS
        cols = pl.ds(pl.multiple_of(group * WIDTH, HEAD), WIDTH)
        packed[step][0:64, :] = query[0, :, cols]
        packed[step][64:128, :] = key[0, :, cols]
        packed[step][128:256, :] = text_key[0, :, cols]
        packed[step][256:320, :] = value[0, :, cols]
        packed[step][320:448, :] = text_value[0, :, cols]


def norm_rows(rows, gain_row):
    rows = rows.astype(f32)
    inverse_rms = lax.rsqrt(jnp.mean(rows * rows, axis=-1, keepdims=True) + epsilon)
    return (rows * inverse_rms * gain_row).astype(bf16)


def matmul(left_side, right_side):
    return jnp.dot(left_side, right_side, preferred_element_type=f32)


def contract_rows(left_side, right_side):
    return lax.dot_general(left_side, right_side, (((1,), (1,)), ((), ())), preferred_element_type=f32)


def attend_body(place, first, second, third, fourth, query_gain, key_gain, attended, pooled):
    packed = (first, second, third, fourth)
    for head in range(3):
        cols = slice(head * HEAD, (head + 1) * HEAD)
        query = jnp.concatenate([packed[s][0:64, cols] for s in range(GROUPS)], axis=0)
        key = jnp.concatenate([packed[s][64:256, cols] for s in range(GROUPS)], axis=0)
        value = jnp.concatenate([packed[s][256:448, cols] for s in range(GROUPS)], axis=0)
        query = norm_rows(query, query_gain[...])
        key = norm_rows(key, key_gain[...])
        exponent = jnp.exp(contract_rows(query, key) * HEAD ** (-0.5))
        total = jnp.sum(exponent, axis=-1, keepdims=True)
        mixed = matmul(exponent.astype(bf16), value) / total
        for step in range(GROUPS):
            source = (place[0] + GROUPS - step) % GROUPS
            rows = pl.ds(pl.multiple_of(source * IMG, IMG), IMG)
            attended[0, rows, cols] = mixed[step * IMG : (step + 1) * IMG].astype(bf16)
    reward_token = lax.broadcasted_iota(jnp.int32, (64, 256), 0)
    token = lax.broadcasted_iota(jnp.int32, (64, 256), 1)
    same_row = (token >> 6) == (reward_token >> 4)
    same_col = ((token & 31) >> 1) == (reward_token & 15)
    pool = jnp.where(same_row & same_col, 0.25, 0.0).astype(bf16)
    pooled[...] = matmul(pool, attended[0]).astype(bf16)


def layer_stats(residual):
    centered = residual - jnp.mean(residual, axis=-1, keepdims=True)
    inverse_std = lax.rsqrt(jnp.mean(centered * centered, axis=-1, keepdims=True) + epsilon)
    return (centered * inverse_std, inverse_std)


def layer_back(upstream, normed, inverse_std):
    return inverse_std * (
        upstream
        - jnp.mean(upstream, axis=-1, keepdims=True)
        - normed * jnp.mean(upstream * normed, axis=-1, keepdims=True)
    )


def embed_body(pooled, embed_weight, position_embed, residual_in, weight, sems):
    def part(group):
        rows = pl.ds(group * WIDTH, WIDTH)
        return pltpu.make_async_copy(embed_weight.at[rows, :], weight.at[rows, :], sems.at[group])

    for group in range(GROUPS):
        part(group).start()
    total = position_embed[...]
    for group in range(GROUPS):
        part(group).wait()
        total = total + matmul(pooled[group], weight[group * WIDTH : (group + 1) * WIDTH, :])
    residual_in[...] = total


def by_core(core, first, second, compute):
    @pl.when(core[0] == 0)
    def _():
        compute(first, second)

    @pl.when(core[0] != 0)
    def _():
        compute(second, first)


def forward_body(core, residual_in, norm_gain, first, second, low, high, derivative_out, hidden):
    normed, _ = layer_stats(residual_in[...])
    hidden[...] = (normed * norm_gain[...]).astype(bf16)

    def compute(up, down):
        preact = contract_rows(hidden[...], up[...])
        cumulative = 0.5 * (1.0 + lax.erf(preact * root_half))
        derivative_out[...] = cumulative + preact * jnp.exp(-0.5 * preact * preact) * inv_root_tau
        part = matmul((preact * cumulative).astype(bf16), down[...]).astype(bf16)
        low[...] = part[0:32]
        high[...] = part[32:64]

    by_core(core, first, second, compute)


def sum_halves(halves):
    low, low_other, high, high_other = halves
    low = low[...].astype(f32) + low_other[...].astype(f32)
    high = high[...].astype(f32) + high_other[...].astype(f32)
    return jnp.concatenate([low, high], axis=0)


def group_sum(low, high):
    inner = [(0, 1), (1, 0), (2, 3), (3, 2)]
    outer = [(0, 3), (3, 0), (1, 2), (2, 1)]

    def pair_sum(mine, other):
        return (mine.astype(f32) + other.astype(f32)).astype(bf16)

    low_pair = lax.ppermute(low, "seq", inner)
    high_pair = lax.ppermute(high, "seq", outer)
    low, high = pair_sum(low, low_pair), pair_sum(high, high_pair)
    return (low, lax.ppermute(low, "seq", outer), high, lax.ppermute(high, "seq", inner))


def backward_body(
    core, residual_in, b0, b1, b2, b3, norm_gain, direction_row, derivative, first, second, embed_rows,
    blocks, reward, out_slope, part, embed_weight, sem,
):
    fetch = pltpu.make_async_copy(embed_rows, embed_weight, sem)
    fetch.start()
    residual_out = residual_in[...] + sum_halves((b0, b1, b2, b3))
    normed, inverse_std = layer_stats(residual_out)
    direction = direction_row[...]
    reward[0] = jnp.sum(normed * direction) * (1.0 / 64.0)
    out_slope[...] = layer_back(direction, normed, inverse_std)

    def compute(up, down):
        back_slope = contract_rows(out_slope[...].astype(bf16), down[...])
        hidden_slope = (back_slope * derivative[...]).astype(bf16)
        part[...] = matmul(hidden_slope, up[...])

    by_core(core, first, second, compute)
    normed, inverse_std = layer_stats(residual_in[...])
    share = layer_back(part[...] * norm_gain[...], normed, inverse_std)
    share = (share + 0.25 * out_slope[...]).astype(bf16)
    fetch.wait()
    for group in range(GROUPS):
        rows = slice(group * WIDTH, (group + 1) * WIDTH)
        blocks[group] = (0.25 * contract_rows(share, embed_weight[rows, :])).astype(bf16)


def finish_body(blocks, gradient):
    pooled_slope = blocks[0].astype(f32)
    for group in range(1, GROUPS):
        pooled_slope = pooled_slope + blocks[group].astype(f32)
    token = lax.broadcasted_iota(jnp.int32, (256, 64), 0)
    reward_token = lax.broadcasted_iota(jnp.int32, (256, 64), 1)
    same_row = (token >> 6) == (reward_token >> 4)
    same_col = ((token & 31) >> 1) == (reward_token & 15)
    spread = jnp.where(same_row & same_col, 1.0, 0.0).astype(bf16)
    gradient[0] = matmul(spread, pooled_slope.astype(bf16)).astype(bf16)


def shape(dims, dtype):
    return jax.ShapeDtypeStruct(dims, dtype)


def held(value):
    return pltpu.with_memory_space_constraint(value, pltpu.VMEM)


def in_any(count):
    return [pl.BlockSpec(memory_space=pl.ANY)] * count


def in_hbm(value):
    return pltpu.with_memory_space_constraint(value, pltpu.HBM)


def in_vmem(count):
    return [pl.BlockSpec(memory_space=pltpu.VMEM)] * count


room = pltpu.CompilerParams(vmem_limit_bytes=16 * 1024 * 1024)
scalar_spec = pl.BlockSpec(memory_space=pltpu.SMEM)


def spread_to(value, axes, count):
    copies = jnp.broadcast_to(value[None], (count, *value.shape))
    return lax.all_to_all(copies, axes, split_axis=0, concat_axis=0, tiled=True)


def on_device(
    image_query, image_key, image_value, text_key, text_value, query_gain, key_gain, embed_weight,
    position_embed, norm_gain, final_gain, up_weight, down_weight, reward_direction,
):
    core = lax.axis_index("core").astype(jnp.int32).reshape(1)
    group = lax.axis_index("seq").astype(jnp.int32).reshape(1)
    packed = pl.pallas_call(
        pack_body,
        out_shape=(
            *(shape((ROWS, WIDTH), bf16),) * GROUPS, shape((1, EMB), f32), shape((1, EMB), f32),
            shape((6, 8, EMB), bf16),
        ),
        in_specs=[scalar_spec, *in_vmem(10)], out_specs=tuple(in_vmem(7)), name="pack",
    )(
        group, image_query, image_key, image_value, text_key, text_value, norm_gain, final_gain,
        reward_direction, up_weight, down_weight,
    )
    *packed, gain_row, direction_row, copies = packed
    nearby = lax.all_to_all(copies, ("zl", "core"), split_axis=0, concat_axis=0, tiled=True)
    nearby_up = nearby[:, 0:4, :].reshape(24, EMB)
    nearby_down = nearby[:, 4:8, :].reshape(24, EMB)
    mine = jnp.where(core[0] == 0, nearby_up, nearby_down)
    mine = spread_to(mine, "y", 8).reshape(192, EMB)
    first = spread_to(mine, "x", 4).reshape(HIDDEN, EMB)
    second = lax.ppermute(first, "core", [(0, 1), (1, 0)])

    received = [packed[0]]
    for step in (2, 1, 3):
        around = [(member, (member + step) % GROUPS) for member in range(GROUPS)]
        received.append(lax.ppermute(packed[step], "seq", around))
    received = [received[0], received[2], received[1], received[3]]
    attended, pooled = pl.pallas_call(
        attend_body, out_shape=(shape((1, 256, WIDTH), bf16), shape((64, WIDTH), bf16)),
        in_specs=[scalar_spec, *in_vmem(6)], out_specs=tuple(in_vmem(2)), name="attend",
    )(group, *map(held, received), query_gain.reshape(1, HEAD), key_gain.reshape(1, HEAD))
    pooled = lax.all_gather(pooled, "seq", axis=0, tiled=False)
    residual_in = pl.pallas_call(
        embed_body, out_shape=shape((64, EMB), f32),
        in_specs=[in_vmem(1)[0], *in_any(1), *in_vmem(1)], out_specs=pl.BlockSpec(memory_space=pltpu.VMEM),
        scratch_shapes=[pltpu.VMEM((1536, EMB), bf16), pltpu.SemaphoreType.DMA((GROUPS,))],
        compiler_params=room, name="embed",
    )(pooled, in_hbm(embed_weight), in_hbm(position_embed))
    half = shape((32, EMB), bf16)
    low, high, derivative = pl.pallas_call(
        forward_body, out_shape=(half, half, shape((64, HIDDEN), f32)),
        in_specs=[scalar_spec, *in_vmem(4)], out_specs=tuple(in_vmem(3)),
        scratch_shapes=[pltpu.VMEM((64, EMB), bf16)], compiler_params=room, name="forward",
    )(core, residual_in, gain_row, held(first), held(second))
    branch = group_sum(low, high)
    blocks, reward = pl.pallas_call(
        backward_body, out_shape=(shape((GROUPS, 64, WIDTH), bf16), shape((1,), f32)),
        in_specs=[scalar_spec, *in_vmem(10), *in_any(1)], out_specs=(in_vmem(1)[0], scalar_spec),
        scratch_shapes=[
            pltpu.VMEM((64, EMB), f32), pltpu.VMEM((64, EMB), f32), pltpu.VMEM((1536, EMB), bf16),
            pltpu.SemaphoreType.DMA,
        ],
        compiler_params=room, name="backward",
    )(
        core, residual_in, *map(held, branch), gain_row, direction_row, derivative, held(first),
        held(second), in_hbm(embed_weight),
    )
    blocks = lax.all_to_all(blocks, "seq", split_axis=0, concat_axis=0, tiled=True)
    gradient = pl.pallas_call(
        finish_body, out_shape=shape((1, 256, WIDTH), bf16), in_specs=in_vmem(1),
        out_specs=pl.BlockSpec(memory_space=pltpu.VMEM), name="finish",
    )(held(blocks))
    return (attended, gradient, reward)


def solution(mesh):
    fine = Mesh(mesh.devices.reshape(4, 8, 3, 2, 4), ("x", "y", "zl", "core", "seq"))
    dp = ("x", "y", "zl", "core")
    return jax.shard_map(
        on_device,
        mesh=fine,
        in_specs=(
            P(dp, "seq", None),
            P(dp, "seq", None),
            P(dp, "seq", None),
            P(dp, "seq", None),
            P(dp, "seq", None),
            P(),
            P(),
            P(),
            P(),
            P(),
            P(),
            P((*dp, "seq"), None),
            P((*dp, "seq"), None),
            P(),
        ),
        out_specs=(P(dp, None, "seq"), P(dp, None, "seq"), P(dp)),
        check_vma=False,
    )
```

```python
import jax
import jax.numpy as jnp
from jax import lax
from jax.experimental import pallas as pl
from jax.experimental.pallas import tpu as pltpu
from jax.sharding import Mesh, PartitionSpec as P


HEAD = 128
IMG, TXT, GROUPS = 64, 128, 4
ROWS = 3 * IMG + 2 * TXT
WIDTH = 384
EMB = 1408
HIDDEN = 768


epsilon = 1e-06
root_half = 0.7071067811865476
inv_root_tau = 0.3989422804014327
f32 = jnp.float32
bf16 = jnp.bfloat16


def pack_body(
    place, query, key, value, text_key, text_value, norm_gain, final_gain, reward_direction, up, down,
    p0, p1, p2, p3, gain_row, direction_row, copies,
):
    rows = jnp.concatenate([up[...], down[...]], axis=0)
    for member in range(6):
        copies[member] = rows
    gain_row[...] = norm_gain[...].reshape(1, EMB)
    direction_row[...] = (final_gain[...] * reward_direction[...]).reshape(1, EMB)
    packed = (p0, p1, p2, p3)
    for step in range(GROUPS):
        group = (place[0] + step) % GROUPS
        cols = pl.ds(pl.multiple_of(group * WIDTH, HEAD), WIDTH)
        packed[step][0:64, :] = query[0, :, cols]
        packed[step][64:128, :] = key[0, :, cols]
        packed[step][128:256, :] = text_key[0, :, cols]
        packed[step][256:320, :] = value[0, :, cols]
        packed[step][320:448, :] = text_value[0, :, cols]


def norm_rows(rows, gain_row):
    rows = rows.astype(f32)
    inverse_rms = lax.rsqrt(jnp.mean(rows * rows, axis=-1, keepdims=True) + epsilon)
    return (rows * inverse_rms * gain_row).astype(bf16)


def matmul(left_side, right_side):
    return jnp.dot(left_side, right_side, preferred_element_type=f32)


def contract_rows(left_side, right_side):
    return lax.dot_general(left_side, right_side, (((1,), (1,)), ((), ())), preferred_element_type=f32)


def attend_body(place, first, second, third, fourth, query_gain, key_gain, attended, pooled):
    packed = (first, second, third, fourth)
    for head in range(3):
        cols = slice(head * HEAD, (head + 1) * HEAD)
        query = jnp.concatenate([packed[s][0:64, cols] for s in range(GROUPS)], axis=0)
        key = jnp.concatenate([packed[s][64:256, cols] for s in range(GROUPS)], axis=0)
        value = jnp.concatenate([packed[s][256:448, cols] for s in range(GROUPS)], axis=0)
        query = norm_rows(query, query_gain[...])
        key = norm_rows(key, key_gain[...])
        exponent = jnp.exp(contract_rows(query, key) * HEAD ** (-0.5))
        total = jnp.sum(exponent, axis=-1, keepdims=True)
        mixed = matmul(exponent.astype(bf16), value) / total
        for step in range(GROUPS):
            source = (place[0] + GROUPS - step) % GROUPS
            rows = pl.ds(pl.multiple_of(source * IMG, IMG), IMG)
            attended[0, rows, cols] = mixed[step * IMG : (step + 1) * IMG].astype(bf16)
    reward_token = lax.broadcasted_iota(jnp.int32, (64, 256), 0)
    token = lax.broadcasted_iota(jnp.int32, (64, 256), 1)
    same_row = (token >> 6) == (reward_token >> 4)
    same_col = ((token & 31) >> 1) == (reward_token & 15)
    pool = jnp.where(same_row & same_col, 0.25, 0.0).astype(bf16)
    pooled[...] = matmul(pool, attended[0]).astype(bf16)


def layer_stats(residual):
    centered = residual - jnp.mean(residual, axis=-1, keepdims=True)
    inverse_std = lax.rsqrt(jnp.mean(centered * centered, axis=-1, keepdims=True) + epsilon)
    return (centered * inverse_std, inverse_std)


def layer_back(upstream, normed, inverse_std):
    return inverse_std * (
        upstream
        - jnp.mean(upstream, axis=-1, keepdims=True)
        - normed * jnp.mean(upstream * normed, axis=-1, keepdims=True)
    )


def embed_body(pooled, embed_weight, position_embed, residual_in, weight, sems):
    def part(group):
        rows = pl.ds(group * WIDTH, WIDTH)
        return pltpu.make_async_copy(embed_weight.at[rows, :], weight.at[rows, :], sems.at[group])

    for group in range(GROUPS):
        part(group).start()
    total = position_embed[...]
    for group in range(GROUPS):
        part(group).wait()
        total = total + matmul(pooled[group], weight[group * WIDTH : (group + 1) * WIDTH, :])
    residual_in[...] = total


def by_core(core, first, second, compute):
    @pl.when(core[0] == 0)
    def _():
        compute(first, second)

    @pl.when(core[0] != 0)
    def _():
        compute(second, first)


def forward_body(core, residual_in, norm_gain, first, second, low, high, derivative_out, hidden):
    normed, _ = layer_stats(residual_in[...])
    hidden[...] = (normed * norm_gain[...]).astype(bf16)

    def compute(up, down):
        preact = contract_rows(hidden[...], up[...])
        cumulative = 0.5 * (1.0 + lax.erf(preact * root_half))
        derivative_out[...] = cumulative + preact * jnp.exp(-0.5 * preact * preact) * inv_root_tau
        part = matmul((preact * cumulative).astype(bf16), down[...]).astype(bf16)
        low[...] = part[0:32]
        high[...] = part[32:64]

    by_core(core, first, second, compute)


def sum_halves(halves):
    low, low_other, high, high_other = halves
    low = low[...].astype(f32) + low_other[...].astype(f32)
    high = high[...].astype(f32) + high_other[...].astype(f32)
    return jnp.concatenate([low, high], axis=0)


def group_sum(low, high):
    inner = [(0, 1), (1, 0), (2, 3), (3, 2)]
    outer = [(0, 3), (3, 0), (1, 2), (2, 1)]

    def pair_sum(mine, other):
        return (mine.astype(f32) + other.astype(f32)).astype(bf16)

    low_pair = lax.ppermute(low, "seq", inner)
    high_pair = lax.ppermute(high, "seq", outer)
    low, high = pair_sum(low, low_pair), pair_sum(high, high_pair)
    return (low, lax.ppermute(low, "seq", outer), high, lax.ppermute(high, "seq", inner))


def backward_body(
    core, residual_in, b0, b1, b2, b3, norm_gain, direction_row, derivative, first, second, embed_rows,
    blocks, reward, out_slope, part, embed_weight, sem,
):
    fetch = pltpu.make_async_copy(embed_rows, embed_weight, sem)
    fetch.start()
    residual_out = residual_in[...] + sum_halves((b0, b1, b2, b3))
    normed, inverse_std = layer_stats(residual_out)
    direction = direction_row[...]
    reward[0] = jnp.sum(normed * direction) * (1.0 / 64.0)
    out_slope[...] = layer_back(direction, normed, inverse_std)

    def compute(up, down):
        back_slope = contract_rows(out_slope[...].astype(bf16), down[...])
        hidden_slope = (back_slope * derivative[...]).astype(bf16)
        part[...] = matmul(hidden_slope, up[...])

    by_core(core, first, second, compute)
    normed, inverse_std = layer_stats(residual_in[...])
    share = layer_back(part[...] * norm_gain[...], normed, inverse_std)
    share = (share + 0.25 * out_slope[...]).astype(bf16)
    fetch.wait()
    for group in range(GROUPS):
        rows = slice(group * WIDTH, (group + 1) * WIDTH)
        blocks[group] = (0.25 * contract_rows(share, embed_weight[rows, :])).astype(bf16)


def finish_body(blocks, gradient):
    pooled_slope = blocks[0].astype(f32)
    for group in range(1, GROUPS):
        pooled_slope = pooled_slope + blocks[group].astype(f32)
    token = lax.broadcasted_iota(jnp.int32, (256, 64), 0)
    reward_token = lax.broadcasted_iota(jnp.int32, (256, 64), 1)
    same_row = (token >> 6) == (reward_token >> 4)
    same_col = ((token & 31) >> 1) == (reward_token & 15)
    spread = jnp.where(same_row & same_col, 1.0, 0.0).astype(bf16)
    gradient[0] = matmul(spread, pooled_slope.astype(bf16)).astype(bf16)


def shape(dims, dtype):
    return jax.ShapeDtypeStruct(dims, dtype)


def held(value):
    return pltpu.with_memory_space_constraint(value, pltpu.VMEM)


def in_any(count):
    return [pl.BlockSpec(memory_space=pl.ANY)] * count


def in_hbm(value):
    return pltpu.with_memory_space_constraint(value, pltpu.HBM)


def in_vmem(count):
    return [pl.BlockSpec(memory_space=pltpu.VMEM)] * count


room = pltpu.CompilerParams(vmem_limit_bytes=16 * 1024 * 1024)
scalar_spec = pl.BlockSpec(memory_space=pltpu.SMEM)


def spread_to(value, axes, count):
    copies = jnp.broadcast_to(value[None], (count, *value.shape))
    return lax.all_to_all(copies, axes, split_axis=0, concat_axis=0, tiled=True)


def on_device(
    image_query, image_key, image_value, text_key, text_value, query_gain, key_gain, embed_weight,
    position_embed, norm_gain, final_gain, up_weight, down_weight, reward_direction,
):
    core = lax.axis_index("core").astype(jnp.int32).reshape(1)
    group = lax.axis_index("seq").astype(jnp.int32).reshape(1)
    packed = pl.pallas_call(
        pack_body,
        out_shape=(
            *(shape((ROWS, WIDTH), bf16),) * GROUPS, shape((1, EMB), f32), shape((1, EMB), f32),
            shape((6, 8, EMB), bf16),
        ),
        in_specs=[scalar_spec, *in_vmem(10)], out_specs=tuple(in_vmem(7)), compiler_params=room, name="pack",
    )(
        group,
        *map(in_hbm, (image_query, image_key, image_value, text_key, text_value, norm_gain, final_gain)),
        in_hbm(reward_direction), in_hbm(up_weight), in_hbm(down_weight),
    )
    *packed, gain_row, direction_row, copies = packed
    nearby = lax.all_to_all(copies, ("zl", "core"), split_axis=0, concat_axis=0, tiled=True)
    nearby_up = nearby[:, 0:4, :].reshape(24, EMB)
    nearby_down = nearby[:, 4:8, :].reshape(24, EMB)
    mine = jnp.where(core[0] == 0, nearby_up, nearby_down)
    mine = spread_to(mine, "y", 8).reshape(192, EMB)
    first = spread_to(mine, "x", 4).reshape(HIDDEN, EMB)
    second = lax.ppermute(first, "core", [(0, 1), (1, 0)])

    received = [packed[0]]
    for step in (2, 1, 3):
        around = [(member, (member + step) % GROUPS) for member in range(GROUPS)]
        received.append(lax.ppermute(packed[step], "seq", around))
    received = [received[0], received[2], received[1], received[3]]
    attended, pooled = pl.pallas_call(
        attend_body, out_shape=(shape((1, 256, WIDTH), bf16), shape((64, WIDTH), bf16)),
        in_specs=[scalar_spec, *in_vmem(6)], out_specs=tuple(in_vmem(2)), compiler_params=room, name="attend",
    )(group, *map(held, received), in_hbm(query_gain.reshape(1, HEAD)), in_hbm(key_gain.reshape(1, HEAD)))
    pooled = lax.all_gather(pooled, "seq", axis=0, tiled=False)
    residual_in = pl.pallas_call(
        embed_body, out_shape=shape((64, EMB), f32),
        in_specs=[in_vmem(1)[0], *in_any(1), *in_vmem(1)], out_specs=pl.BlockSpec(memory_space=pltpu.VMEM),
        scratch_shapes=[pltpu.VMEM((1536, EMB), bf16), pltpu.SemaphoreType.DMA((GROUPS,))],
        compiler_params=room, name="embed",
    )(pooled, in_hbm(embed_weight), in_hbm(position_embed))
    half = shape((32, EMB), bf16)
    low, high, derivative = pl.pallas_call(
        forward_body, out_shape=(half, half, shape((64, HIDDEN), f32)),
        in_specs=[scalar_spec, *in_vmem(4)], out_specs=tuple(in_vmem(3)),
        scratch_shapes=[pltpu.VMEM((64, EMB), bf16)], compiler_params=room, name="forward",
    )(core, residual_in, gain_row, held(first), held(second))
    branch = group_sum(low, high)
    blocks, reward = pl.pallas_call(
        backward_body, out_shape=(shape((GROUPS, 64, WIDTH), bf16), shape((1,), f32)),
        in_specs=[scalar_spec, *in_vmem(10), *in_any(1)], out_specs=(in_vmem(1)[0], scalar_spec),
        scratch_shapes=[
            pltpu.VMEM((64, EMB), f32), pltpu.VMEM((64, EMB), f32), pltpu.VMEM((1536, EMB), bf16),
            pltpu.SemaphoreType.DMA,
        ],
        compiler_params=room, name="backward",
    )(
        core, residual_in, *map(held, branch), gain_row, direction_row, derivative, held(first),
        held(second), in_hbm(embed_weight),
    )
    blocks = lax.all_to_all(blocks, "seq", split_axis=0, concat_axis=0, tiled=True)
    gradient = pl.pallas_call(
        finish_body, out_shape=shape((1, 256, WIDTH), bf16), in_specs=in_vmem(1),
        out_specs=pl.BlockSpec(memory_space=pltpu.VMEM), compiler_params=room, name="finish",
    )(held(blocks))
    return (attended, gradient, reward)


def solution(mesh):
    fine = Mesh(mesh.devices.reshape(4, 8, 3, 2, 4), ("x", "y", "zl", "core", "seq"))
    dp = ("x", "y", "zl", "core")
    return jax.shard_map(
        on_device,
        mesh=fine,
        in_specs=(
            P(dp, "seq", None),
            P(dp, "seq", None),
            P(dp, "seq", None),
            P(dp, "seq", None),
            P(dp, "seq", None),
            P(),
            P(),
            P(),
            P(),
            P(),
            P(),
            P((*dp, "seq"), None),
            P((*dp, "seq"), None),
            P(),
        ),
        out_specs=(P(dp, None, "seq"), P(dp, None, "seq"), P(dp)),
        check_vma=False,
    )
```
